256 devices in a mesh: ctx: 16 (over z_lo, x, core), head: 16 (over y, z_hi).
Axes of the slice: x: 4, y: 4, z: 8 (z_hi: 4, z_lo: 2; z = z_hi * 2 + z_lo), core: 2. Of those that a mesh axis runs over, the one named last changes fastest.
Arguments:
- layer_input: bfloat16 [4096, 8192], P('ctx'), may hold values from -6 to 6
- output_grad: bfloat16 [4096, 8192], P('ctx'), may hold values from -6 to 6
- routes: int32 [4096, 8], P('ctx'), may hold values from 0 to 63, all different within a row; in each aligned block of 256 rows (0 to 255, 256 to 511, ...) at most 64 rows name the same one
- route_gates: float32 [4096, 8], P('ctx'), may hold values from 0.05 to 0.3
- query_weight: bfloat16 [80, 8192, 128], P('head', 'ctx'), may hold values from -0.0625 to 0.0625
- output_weight: bfloat16 [80, 8192, 128], P('head', 'ctx'), may hold values from -0.0625 to 0.0625
- key_values: bfloat16 [16, 4096, 128], P('head', 'ctx'), may hold values from -96 to 96
Outputs:
- input_grad: bfloat16 [4096, 8192], P('ctx', 'head')
- keyvalue_grad: float32 [16, 4096, 128], P('head', 'ctx')
The draws below stay inside these ranges and needn't reach their ends.
Inputs may be any that keep to these rules, and one draw needn't show every extreme that they name: `routes`: each row names 8 different experts; in the 256 rows of one ctx block no expert is named more than 64 times, and some expert reaches 64.
All inputs are finite; a program needn't handle non-finite values.
Results may differ from the reference program's by a relative error of at most 0.015.
The reference program's roundings to bfloat16 on the way count: a program that leaves them out, or rounds other values in their place, can miss the bound.
Values may be sent and summed in bfloat16 or wider, within the bound.
No kernel may reach another device: no remote copies, remote signals or barrier semaphores. Data moves between devices by JAX's collectives and lax.ppermute only.
A program may use at most 128 MiB of HBM per device.

```python
import math
import jax
import jax.numpy as jnp
import numpy as np
from jax import lax

D = 8192
HD = 128
TOP = 8
EXP_DEV = 4
TOK_DEV = 256
EXPERTS = 64
HEADS = 80
KVG = 8
CAP = 64
TOKENS = 4096
N_CTX = 16
N_HEAD = 16


def draw_key_values(key, part):
    normal_draw = jax.random.normal(key, (2 * KVG, TOKENS, HD), jnp.float32)
    normal_draw = jnp.clip(normal_draw, -4.0, 4.0)
    return normal_draw.astype(jnp.bfloat16)


def block_scale(own_key, extent, pieces, smallest, top_value):
    gain = 1.0
    for position, parts in pieces:
        draws = jax.random.uniform(jax.random.fold_in(jax.random.fold_in(own_key, 6), position), (parts,), jnp.float32, smallest / len(pieces), top_value / len(pieces))
        gain = gain * jnp.repeat(jnp.exp(draws), extent[position] // parts).reshape((-1,) + (1,) * (len(extent) - 1 - position))
    return gain


def assign_block(stream_key, own, number, rows, number_of, top, bound, skew):
    order = jax.random.permutation(stream_key, number_of)
    crowded, common = portions_of(number_of, rows * top, bound, skew, True), portions_of(number_of, rows * top, bound, skew, False)
    places = jnp.arange(number_of)

    def named(tallies, turn):
        used = int((tallies > 0).sum())
        fixed = max(1, used // 4)
        moved = fixed + (places - fixed + turn * (used - fixed)) % max(1, number_of - fixed)
        return jnp.zeros((number_of,), jnp.int32).at[order[jnp.where(places < fixed, places, moved)]].set(jnp.asarray(tallies, jnp.int32))

    tallies = jnp.where(number % 4 == 0, named(crowded, number // 4), named(common, number - number // 4 - 1))
    mixed = jax.random.permutation(jax.random.fold_in(own, 3), number_of)
    giver, receiver = mixed[0:number_of // 2 * 2:2], mixed[1:number_of // 2 * 2:2]
    margin = jnp.minimum(tallies[giver] - 1, bound - tallies[receiver]) // 2
    margin = jnp.where((giver == order[0]) | (receiver == order[0]) | (tallies[receiver] == 0), 0, jnp.maximum(margin, 0))
    moved = jax.random.randint(jax.random.fold_in(own, 4), (number_of // 2,), 0, 1 << 20) % (margin + 1)
    tallies = tallies.at[giver].add(-moved).at[receiver].add(moved)
    items = jnp.searchsorted(jnp.cumsum(tallies), jnp.arange(rows * top), side="right").astype(jnp.int32)
    listing = items.reshape(top, rows).T
    listing = listing[jax.random.permutation(jax.random.fold_in(own, 1), rows)]
    turn = jax.random.randint(jax.random.fold_in(own, 2), (rows, 1), 0, top)
    return jnp.take_along_axis(listing, (jnp.arange(top)[None, :] + turn) % top, axis=1)


def portions_of(number_of, total, most, lean, full):
    loads = [(1 << 20) // math.isqrt(standing ** lean) + 1 for standing in range(1, number_of + 1)]
    largest = most if full else min(most, max(-(-total // number_of), total * loads[0] // sum(loads)))
    least = 1 if total - largest >= number_of - 1 else 0
    counts, surplus = [largest] + [least] * (number_of - 1), total - largest - least * (number_of - 1)
    while surplus > 0:
        movable = [i for i in range(1, number_of) if counts[i] < largest] or [i for i in range(1, number_of) if counts[i] < most]
        whole, left = sum([loads[i] for i in movable]), surplus
        for i in movable:
            extra = min(most - counts[i], max(1, left * loads[i] // whole), surplus)
            counts[i] = counts[i] + extra
            surplus = surplus - extra
    return np.array(counts)


def scatter_about(rng, dims, deviation, limit, shards=(), kind=jnp.bfloat16):
    entries = deviation * jax.random.normal(rng, dims, jnp.float32)
    if shards:
        entries = entries * block_scale(rng, dims, shards, -0.22, 0.18)
    return jnp.clip(entries, -limit, limit).astype(kind)


def setup_inputs(seed: int = 0) -> dict:
    streams_of = jax.random.split(jax.random.key(seed), 8)
    layer_input = scatter_about(streams_of[0], (TOKENS, D), 1.0, 6.0, ((0, 16),))
    output_grad = scatter_about(streams_of[1], (TOKENS, D), 1.0, 6.0, ((0, 16),))
    routes_keys = jax.random.split(jax.random.fold_in(streams_of[2], 1), TOKENS // TOK_DEV)
    routes_turns = jax.random.permutation(jax.random.fold_in(streams_of[2], 3), TOKENS // TOK_DEV)
    routes = jax.vmap(lambda own, number: assign_block(jax.random.fold_in(streams_of[2], 2), own, number, TOK_DEV, EXPERTS, TOP, CAP, 2))(routes_keys, routes_turns).reshape((TOKENS, TOP))
    route_gates = jnp.clip(0.05 + 0.25 * jax.random.uniform(streams_of[3], (TOKENS, TOP), jnp.float32) ** block_scale(streams_of[3], (TOKENS, TOP), ((0, 16),), -0.2, 0.2), 0.05, 0.3)
    query_weight = scatter_about(streams_of[4], (HEADS, D, HD), D ** -0.5, 0.0625, ((0, 16), (1, 16)))
    output_weight = scatter_about(streams_of[5], (HEADS, D, HD), D ** -0.5, 0.0625, ((0, 16), (1, 16)))
    key_values = draw_key_values(jax.random.fold_in(streams_of[7], 71), 0)
    return dict(layer_input=layer_input, output_grad=output_grad, routes=routes, route_gates=route_gates, query_weight=query_weight, output_weight=output_weight, key_values=key_values)


PRECISE = lax.Precision.HIGHEST


def slot_table(route_rows, first_id, expert_count, slot_count):
    expert_ids = first_id + jnp.arange(expert_count, dtype=jnp.int32)
    matches = route_rows[:, :, None] == expert_ids[None, None, :]
    member = jnp.any(matches, axis=1).astype(jnp.int32)
    placed = jnp.cumsum(member, axis=0) - 1
    slot_map = (placed.T[:, None, :] == jnp.arange(slot_count, dtype=jnp.int32)[None, :, None]) & (member.T[:, None, :] == 1)
    return slot_map.astype(jnp.float32)


def expert_gate(route_rows, gate_rows, first_id, expert_count):
    expert_ids = first_id + jnp.arange(expert_count, dtype=jnp.int32)
    matches = route_rows[:, :, None] == expert_ids[None, None, :]
    return jnp.sum(jnp.where(matches, gate_rows[:, :, None], jnp.zeros_like(gate_rows)[:, :, None]), axis=1)


def attend(queries, query_place, key_rows, value_rows, key_place, head_grads):
    score_scale = queries.shape[1] ** -0.5
    scores = jnp.dot(queries, key_rows.T, preferred_element_type=jnp.float32) * score_scale
    scores = jnp.where(key_place[None, :] <= query_place[:, None], scores, -1e30)
    row_max = jnp.max(scores, axis=1, keepdims=True)
    raised = jnp.exp(scores - row_max)
    shares = raised / jnp.sum(raised, axis=1, keepdims=True)
    shares_low = shares.astype(jnp.bfloat16)
    outputs = jnp.dot(shares_low, value_rows, preferred_element_type=jnp.float32)
    share_grad = jnp.dot(head_grads, value_rows.T, preferred_element_type=jnp.float32)
    row_delta = jnp.sum(head_grads.astype(jnp.float32) * outputs, axis=1, keepdims=True)
    score_grad = (shares * (share_grad - row_delta) * score_scale).astype(jnp.bfloat16)
    query_grad = jnp.dot(score_grad, key_rows, preferred_element_type=jnp.float32).astype(jnp.bfloat16)
    key_grad = jnp.dot(score_grad.T, queries, preferred_element_type=jnp.float32)
    value_grad = jnp.dot(shares_low.T, head_grads, preferred_element_type=jnp.float32)
    return query_grad, key_grad, value_grad


def reference(layer_input, output_grad, routes, route_gates, query_weight, output_weight, key_values):
    per_block = EXP_DEV + 1
    key_place = jnp.arange(TOKENS, dtype=jnp.int32).astype(jnp.float32)
    place_blocks = key_place.reshape(N_CTX, TOK_DEV)
    input_blocks = layer_input.reshape(N_CTX, TOK_DEV, D).astype(jnp.float32)
    cotan_blocks = output_grad.reshape(N_CTX, TOK_DEV, D).astype(jnp.float32)
    route_blocks = routes.reshape(N_CTX, TOK_DEV, TOP)
    gate_blocks = route_gates.reshape(N_CTX, TOK_DEV, TOP)
    routed_rows = N_CTX * EXP_DEV * CAP

    def head_step(carry, head_index):
        input_acc, pair_acc = carry
        query_block = lax.dynamic_slice_in_dim(query_weight, head_index * per_block, per_block, 0).astype(jnp.float32)
        output_block = lax.dynamic_slice_in_dim(output_weight, head_index * per_block, per_block, 0).astype(jnp.float32)
        group_id = head_index // 2
        key_rows = lax.dynamic_index_in_dim(key_values, 2 * group_id, 0, keepdims=False)
        value_rows = lax.dynamic_index_in_dim(key_values, 2 * group_id + 1, 0, keepdims=False)
        first_id = head_index * EXP_DEV
        tables = jax.vmap(slot_table, in_axes=(0, None, None, None))(route_blocks, first_id, EXP_DEV, CAP)
        token_gates = jax.vmap(expert_gate, in_axes=(0, 0, None, None))(route_blocks, gate_blocks, first_id, EXP_DEV)
        picked_input = jnp.einsum('bjct,btd->bjcd', tables, input_blocks, precision=PRECISE).astype(jnp.bfloat16)
        routed_query = jnp.einsum('bjcd,jde->bjce', picked_input.astype(jnp.float32), query_block[:EXP_DEV], precision=PRECISE).astype(jnp.bfloat16)
        shared_query = jnp.einsum('btd,de->bte', input_blocks, query_block[EXP_DEV], precision=PRECISE).astype(jnp.bfloat16)
        picked_cotan = jnp.einsum('bjct,btd->bjcd', tables, cotan_blocks, precision=PRECISE).astype(jnp.bfloat16)
        slot_gate = jnp.einsum('bjct,btj->bjc', tables, token_gates, precision=PRECISE)
        routed_sum = jnp.einsum('bjcd,jde->bjce', picked_cotan.astype(jnp.float32), output_block[:EXP_DEV], precision=PRECISE)
        routed_cotan = (slot_gate[..., None] * routed_sum).astype(jnp.bfloat16)
        shared_cotan = jnp.einsum('btd,de->bte', cotan_blocks, output_block[EXP_DEV], precision=PRECISE).astype(jnp.bfloat16)
        routed_place = jnp.einsum('bjct,bt->bjc', tables, place_blocks, precision=PRECISE)
        queries = jnp.concatenate([routed_query.reshape(-1, HD), shared_query.reshape(-1, HD)], axis=0)
        query_place = jnp.concatenate([routed_place.reshape(-1), place_blocks.reshape(-1)], axis=0)
        head_grads = jnp.concatenate([routed_cotan.reshape(-1, HD), shared_cotan.reshape(-1, HD)], axis=0)
        query_grad, key_grad, value_grad = attend(queries, query_place, key_rows, value_rows, key_place, head_grads)
        routed_qgrad = query_grad[:routed_rows].reshape(N_CTX, EXP_DEV, CAP, HD).astype(jnp.float32)
        token_qgrad = jnp.einsum('bjct,bjce->btje', tables, routed_qgrad, precision=PRECISE).astype(jnp.bfloat16)
        shared_qgrad = query_grad[routed_rows:].reshape(N_CTX, TOK_DEV, 1, HD)
        every_qgrad = jnp.concatenate([token_qgrad, shared_qgrad], axis=2).reshape(TOKENS, per_block, HD)
        input_acc = input_acc + jnp.einsum('tje,jde->td', every_qgrad.astype(jnp.float32), query_block, precision=PRECISE)
        pair_acc = pair_acc.at[2 * group_id].add(key_grad).at[2 * group_id + 1].add(value_grad)
        return (input_acc, pair_acc), None

    initial = (jnp.zeros((TOKENS, D), jnp.float32), jnp.zeros((2 * KVG, TOKENS, HD), jnp.float32))
    (input_acc, pair_acc), ignored = lax.scan(head_step, initial, jnp.arange(N_HEAD, dtype=jnp.int32))
    return input_acc.astype(jnp.bfloat16), pair_acc
```

```python
import functools

import jax
import jax.numpy as jnp
from jax import lax
from jax.experimental import pallas as pl
from jax.experimental.pallas import tpu as pltpu
from jax.sharding import PartitionSpec as P

F32 = jnp.float32
BF16 = jnp.bfloat16
VMEM_LIMIT = 56 * 2**20
LOG2E = 1.4426950408889634

NX, NY, NZ = 4, 4, 4


def ctx_id(z, x, k):
    return z * 2 * NX + (x % NX) * 2 + k


def ctx_moves(target):
    return [
        (ctx_id(z, x, k), target(z, x, k)) for z in range(2) for x in range(NX) for k in range(2)
    ]


X_UP = ctx_moves(lambda z, x, k: ctx_id(z, x + 1, k))
X_DOWN = ctx_moves(lambda z, x, k: ctx_id(z, x - 1, k))
Z_PAIR = ctx_moves(lambda z, x, k: ctx_id(1 - z, x, k))
CORES = ctx_moves(lambda z, x, k: ctx_id(z, x, 1 - k))


def head_moves(dy, dz):
    return [
        (y * NZ + z, ((y + dy) % NY) * NZ + (z + dz) % NZ) for y in range(NY) for z in range(NZ)
    ]


HEAD_PAIR = [(h, h ^ 1) for h in range(NY * NZ)]


def ctx_send(value, moves):
    return lax.ppermute(value, "ctx", moves)


def head_send(value, dy, dz):
    return lax.ppermute(value, "head", head_moves(dy, dz))


def chip_gather(own):
    half = own.shape[0] // 2
    left = ctx_send(own, X_UP)
    right = ctx_send(own, X_DOWN)
    below = ctx_send(own, Z_PAIR)
    far_a = ctx_send(left[:half], X_UP)
    far_b = ctx_send(right[half:], X_DOWN)
    return {
        (0, 0): (own,),
        (0, -1): (left,),
        (0, 1): (right,),
        (1, 0): (below,),
        (0, 2): (far_a, far_b),
        (1, -1): (ctx_send(below, X_UP),),
        (1, 1): (ctx_send(below, X_DOWN),),
        (1, 2): (ctx_send(far_a, Z_PAIR), ctx_send(far_b, Z_PAIR)),
    }


def both_cores(pieces):
    out = {}
    for (dz, dx), parts in pieces.items():
        out[dz, dx, 0] = parts
        out[dz, dx, 1] = tuple(ctx_send(p, CORES) for p in parts)
    return out


GROUPS = (
    ((0, 0), (0, -1), (0, 1), (1, 0)),
    ((0, 2),),
    ((1, -1), (1, 1), (1, 2)),
)


def project_kernel(layout, heads, depth, keep, first, order_ref, *refs):
    count = len(layout)
    xs, refs = refs[:count], refs[count:]
    total = sum(len(p) for p in layout)
    flat, refs = refs[:total], refs[total:]
    acc_in = None
    if not first:
        acc_in, refs = refs[0], refs[2:]
    acc, stack, sems = refs
    parts, at = [], 0
    for rows in layout:
        here, begin = [], 0
        for r in rows:
            here.append((flat[at], begin, begin + r))
            at, begin = at + 1, begin + r
        parts.append(here)
    copies = []
    for i, here in enumerate(parts):
        for ref, begin, end in here:
            lo, hi = max(begin, keep[0]), min(end, keep[1])
            if lo < hi:
                copies.append(
                    pltpu.make_async_copy(
                        ref.at[pl.ds(lo - begin, hi - lo)],
                        stack.at[order_ref[i], pl.ds(lo - keep[0], hi - lo)],
                        sems.at[len(copies)],
                    )
                )
                copies[-1].start()
    for j in range(heads):
        columns = pl.ds(j * 128, 128)
        total = None if first else acc_in[:, columns]
        for i, here in enumerate(parts):
            for ref, begin, end in here:
                lo, hi = max(begin, j * depth), min(end, (j + 1) * depth)
                if lo < hi:
                    term = jnp.dot(
                        xs[i][:, pl.ds(lo - j * depth, hi - lo)],
                        ref[pl.ds(lo - begin, hi - lo), :],
                        preferred_element_type=F32,
                    )
                    total = term if total is None else total + term
        acc[:, columns] = total
    for copy in copies:
        copy.wait()


def project(x, pieces, order, state, heads, keep, blocks):
    tokens, depth = x.shape[0], x.shape[1] // blocks
    layout = tuple(tuple(p.shape[0] for p in parts) for parts in pieces)
    flat = [p for parts in pieces for p in parts]
    first = state is None
    count = len(pieces)
    whole = pl.BlockSpec(memory_space=pltpu.VMEM)
    anywhere = pl.BlockSpec(memory_space=pl.ANY)
    x_specs = [
        pl.BlockSpec((tokens, depth), functools.partial(lambda g, o, i: (0, o[i]), i=i))
        for i in range(count)
    ]
    n_in = 1 + count + len(flat)
    return pl.pallas_call(
        functools.partial(project_kernel, layout, heads, depth, keep, first),
        grid_spec=pltpu.PrefetchScalarGridSpec(
            num_scalar_prefetch=1,
            grid=(1,),
            in_specs=x_specs + [whole] * len(flat) + ([] if first else [whole, anywhere]),
            out_specs=[whole, anywhere],
            scratch_shapes=[pltpu.SemaphoreType.DMA((len(flat),))],
        ),
        out_shape=[
            jax.ShapeDtypeStruct((tokens, heads * 128), F32),
            jax.ShapeDtypeStruct((blocks, keep[1] - keep[0], 128), BF16),
        ],
        input_output_aliases={} if first else {n_in: 0, n_in + 1: 1},
        compiler_params=pltpu.CompilerParams(vmem_limit_bytes=VMEM_LIMIT),
        name="project",
    )(order, *([x] * count), *flat, *(() if first else state))


def gathered_projection(x, pieces, block_of, heads, keep, blocks):
    state = None
    for group in GROUPS:
        names = [(dz, dx, dk) for dz, dx in group for dk in range(2)]
        order = jnp.stack([block_of(*n) for n in names])
        state = project(x, [pieces[n] for n in names], order, state, heads, keep, blocks)
    return state


NT = (((1,), (1,)), ((), ()))


def attention_kernel(
    slots, here_ref, q_acc, da_acc, gates, pick, unpick, place, kv, dq_out, dkv_out,
    scores, grads, keys_t,
):
    experts = gates.shape[1]
    width = 128
    tokens = q_acc.shape[0]
    routed = experts * slots
    here = here_ref[0]
    scale = width**-0.5
    q_parts, da_parts = [], []
    for j in range(experts):
        columns = pl.ds(j * width, width)
        rows = pl.ds(j * slots, slots)
        q_tok = q_acc[:, columns].astype(BF16)
        da_tok = (gates[:, pl.ds(j, 1)] * da_acc[:, columns]).astype(BF16)
        q_parts.append(jnp.dot(pick[rows, :], q_tok, preferred_element_type=F32))
        da_parts.append(jnp.dot(pick[rows, :], da_tok, preferred_element_type=F32))
    shared = pl.ds(experts * width, width)
    q = jnp.concatenate(q_parts + [q_acc[:, shared]], axis=0).astype(BF16)
    da = jnp.concatenate(da_parts + [da_acc[:, shared]], axis=0).astype(BF16)
    count = q.shape[0]
    places = place[...]

    def score(b, masked):
        k = kv[b, pl.ds(0, tokens), :]
        s = lax.dot_general(k, q, NT, preferred_element_type=F32)
        if masked:
            row = b * tokens + lax.broadcasted_iota(jnp.int32, s.shape, 0)
            s = jnp.where(row <= places, s, -1e30)
        scores[b] = s
        grads[b] = lax.dot_general(
            kv[b, pl.ds(tokens, tokens), :], da, NT, preferred_element_type=F32
        )
        keys_t[b] = k.T
        return jnp.max(s, axis=0, keepdims=True)

    top = score(here, True)
    top = lax.fori_loop(0, here, lambda b, t: jnp.maximum(t, score(b, False)), top)

    def raise_(b, norm):
        e = jnp.exp2((scores[b] - top) * (scale * LOG2E))
        scores[b] = e
        return norm + jnp.sum(e, axis=0, keepdims=True)

    norm = lax.fori_loop(0, here + 1, raise_, jnp.zeros((1, count), F32))
    inverse = 1.0 / norm

    def values(b, delta):
        w = scores[b] * inverse
        low = w.astype(BF16)
        scores[b] = w
        dkv_out[b, pl.ds(tokens, tokens), :] = jnp.dot(
            low, da, preferred_element_type=F32
        ).astype(BF16)
        return delta + jnp.sum(low.astype(F32) * grads[b], axis=0, keepdims=True)

    delta = lax.fori_loop(0, here + 1, values, jnp.zeros((1, count), F32))

    def keys(b, dq_t):
        ds = (scores[b] * (grads[b] - delta) * scale).astype(BF16)
        dkv_out[b, pl.ds(0, tokens), :] = jnp.dot(ds, q, preferred_element_type=F32).astype(BF16)
        return dq_t + jnp.dot(keys_t[b], ds, preferred_element_type=F32)

    dq_t = lax.fori_loop(0, here + 1, keys, jnp.zeros((width, count), F32))

    def blank(b, carry):
        dkv_out[b] = jnp.zeros(dkv_out.shape[1:], BF16)
        return carry

    lax.fori_loop(here + 1, dkv_out.shape[0], blank, 0)
    dq = dq_t.T.astype(BF16)
    for j in range(experts):
        dq_out[:, pl.ds(j * width, width)] = jnp.dot(
            unpick[:, pl.ds(j * slots, slots)],
            dq[j * slots : (j + 1) * slots],
            preferred_element_type=F32,
        ).astype(BF16)
    dq_out[:, shared] = dq[routed:]


def attention(slots, here, q_acc, da_acc, gates, pick, place, kv):
    tokens, blocks = q_acc.shape[0], kv.shape[0]
    count = place.shape[1]
    whole = pl.BlockSpec(memory_space=pltpu.VMEM)
    return pl.pallas_call(
        functools.partial(attention_kernel, slots),
        in_specs=[pl.BlockSpec(memory_space=pltpu.SMEM)] + [whole] * 7,
        out_specs=[whole, whole],
        out_shape=[
            jax.ShapeDtypeStruct(q_acc.shape, BF16),
            jax.ShapeDtypeStruct((blocks, 2 * tokens, 128), BF16),
        ],
        scratch_shapes=[
            pltpu.VMEM((blocks, tokens, count), F32),
            pltpu.VMEM((blocks, tokens, count), F32),
            pltpu.VMEM((blocks, 128, tokens), BF16),
        ],
        compiler_params=pltpu.CompilerParams(vmem_limit_bytes=VMEM_LIMIT),
        name="attention",
    )(here, q_acc, da_acc, gates, pick, pick.T, place, kv)


def back_kernel(heads, depth, order_ref, dq, w, out):
    total = None
    for j in range(heads):
        term = lax.dot_general(
            dq[:, pl.ds(j * 128, 128)],
            w[0, pl.ds(j * depth, depth), :],
            NT,
            preferred_element_type=F32,
        )
        total = term if total is None else total + term
    out[0] = total.astype(BF16)


def back_project(dq, stack, order, heads):
    tokens, depth, count = dq.shape[0], stack.shape[1] // heads, order.shape[0]
    return pl.pallas_call(
        functools.partial(back_kernel, heads, depth),
        grid_spec=pltpu.PrefetchScalarGridSpec(
            num_scalar_prefetch=1,
            grid=(count,),
            in_specs=[
                pl.BlockSpec(dq.shape, lambda i, o: (0, 0)),
                pl.BlockSpec((1,) + stack.shape[1:], lambda i, o: (o[i], 0, 0)),
            ],
            out_specs=pl.BlockSpec((1, tokens, depth), lambda i, o: (i, 0, 0)),
        ),
        out_shape=jax.ShapeDtypeStruct((count, tokens, depth), BF16),
        compiler_params=pltpu.CompilerParams(vmem_limit_bytes=VMEM_LIMIT),
        name="back_project",
    )(order, dq, stack)


def plus(*terms):
    return sum(t.astype(F32) for t in terms)


def ring_sum(far, up, down, own, send):
    up_b = send(up[1], 1)
    down_a = send(down[0], -1)
    far_a = send(far[0], 1)
    far_b = send(far[1], -1)
    up_a = send(plus(up[0], far_a).astype(BF16), 1)
    down_b = send(plus(down[1], far_b).astype(BF16), -1)
    return plus(own[0], up_a, down_a), plus(own[1], up_b, down_b)


def per_device(
    layer_input, output_grad, routes, route_gates, query_weight, output_weight, key_values
):
    tokens = layer_input.shape[0]
    heads = query_weight.shape[0]
    experts = heads - 1
    depth, width = query_weight.shape[1:]
    blocks = lax.axis_size("ctx")
    head_count = lax.axis_size("head")
    slots = 2 * tokens * routes.shape[1] // (experts * head_count)
    c = lax.axis_index("ctx")
    h = lax.axis_index("head")
    z, x, k = c // (2 * NX), (c // 2) % NX, c % 2
    y, zh = h // NZ, h % NZ
    is_even = h % 2 == 0

    def block_of(dz, dx, dk):
        return ctx_id(z ^ dz, x + dx + NX, k ^ dk).astype(jnp.int32)

    query_piece = query_weight.reshape(heads * depth, width)
    query_pieces = both_cores(chip_gather(query_piece))
    own_rows = key_values[0]
    partner_rows = lax.ppermute(own_rows, "head", HEAD_PAIR)
    output_piece = jnp.concatenate(
        [
            output_weight.reshape(heads * depth, width),
            jnp.where(is_even, own_rows, partner_rows),
            jnp.where(is_even, partner_rows, own_rows),
        ],
        axis=0,
    )
    output_pieces = both_cores(chip_gather(output_piece))

    ids = h * experts + jnp.arange(experts, dtype=jnp.int32)
    matches = routes[:, :, None] == ids[None, None, :]
    member = jnp.any(matches, axis=1)
    gates = jnp.sum(jnp.where(matches, route_gates[:, :, None], 0.0), axis=1)
    index = jnp.arange(tokens, dtype=jnp.int32)
    before = (index[None, :] <= index[:, None]).astype(BF16)
    placed = jnp.dot(before, member.astype(BF16), preferred_element_type=F32)
    placed = placed.astype(jnp.int32) - 1
    table = (placed.T[:, None, :] == jnp.arange(slots, dtype=jnp.int32)[None, :, None]) & (
        member.T[:, None, :]
    )
    token_place = c * tokens + index
    routed_place = jnp.max(jnp.where(table, token_place[None, None, :], c * tokens), axis=2)
    place = jnp.concatenate([routed_place.reshape(-1), token_place])[None, :]
    pick = table.reshape(experts * slots, tokens).astype(BF16)

    rows = heads * depth
    q_acc, query_stack = gathered_projection(
        layer_input, query_pieces, block_of, heads, (0, rows), blocks
    )
    da_acc, kv_stack = gathered_projection(
        output_grad, output_pieces, block_of, heads, (rows, rows + 2 * tokens), blocks
    )
    dq, dkv = attention(
        slots, c.astype(jnp.int32)[None], q_acc, da_acc, gates, pick, place, kv_stack
    )

    z_order = (zh + jnp.array([2, 1, 3, 0], jnp.int32)) % NZ

    def term(dy):
        order = ((y + dy) % NY) * NZ + z_order
        return back_project(dq, query_stack, order.astype(jnp.int32), heads)

    def parts(group):
        return group[:2], group[2:]

    first, second = ring_sum(
        parts(term(2)),
        parts(term(1)),
        parts(term(3)),
        parts(term(0)),
        lambda v, d: head_send(v, d, 0),
    )
    half = tokens // 2

    def row_parts(value):
        return value[:half], value[half:]

    low_first, low_down = first.astype(BF16), second[0].astype(BF16)
    top, bottom = ring_sum(
        row_parts(low_first[0]),
        row_parts(low_first[1]),
        row_parts(low_down),
        row_parts(second[1]),
        lambda v, d: head_send(v, 0, d),
    )
    input_grad = jnp.concatenate([top, bottom], axis=0).astype(BF16)

    arrived = lax.all_to_all(dkv, "ctx", split_axis=0, concat_axis=0, tiled=True)
    summed = jnp.sum(arrived.astype(F32), axis=0)
    key_rows, value_rows = summed[:tokens], summed[tokens:]
    incoming = lax.ppermute(jnp.where(is_even, value_rows, key_rows), "head", HEAD_PAIR)
    kept = jnp.where(is_even, key_rows, value_rows) + incoming
    return input_grad, kept[None]


def solution(mesh):
    in_specs = (
        P("ctx", None),
        P("ctx", None),
        P("ctx", None),
        P("ctx", None),
        P("head", "ctx", None),
        P("head", "ctx", None),
        P("head", "ctx", None),
    )
    out_specs = (P("ctx", "head"), P("head", "ctx", None))
    return jax.shard_map(
        per_device, mesh=mesh, in_specs=in_specs, out_specs=out_specs, check_vma=False
    )
```

```python
import functools

import jax
import jax.numpy as jnp
from jax import lax
from jax.experimental import pallas as pl
from jax.experimental.pallas import tpu as pltpu
from jax.sharding import PartitionSpec as P

F32 = jnp.float32
BF16 = jnp.bfloat16
VMEM_LIMIT = 56 * 2**20
LOG2E = 1.4426950408889634

NX, NY, NZ = 4, 4, 4


def ctx_id(z, x, k):
    return z * 2 * NX + (x % NX) * 2 + k


def ctx_moves(target):
    return [
        (ctx_id(z, x, k), target(z, x, k)) for z in range(2) for x in range(NX) for k in range(2)
    ]


X_UP = ctx_moves(lambda z, x, k: ctx_id(z, x + 1, k))
X_DOWN = ctx_moves(lambda z, x, k: ctx_id(z, x - 1, k))
Z_PAIR = ctx_moves(lambda z, x, k: ctx_id(1 - z, x, k))
CORES = ctx_moves(lambda z, x, k: ctx_id(z, x, 1 - k))


def head_moves(dy, dz):
    return [
        (y * NZ + z, ((y + dy) % NY) * NZ + (z + dz) % NZ) for y in range(NY) for z in range(NZ)
    ]


HEAD_PAIR = [(h, h ^ 1) for h in range(NY * NZ)]


def ctx_send(value, moves):
    return lax.ppermute(value, "ctx", moves)


def after(value, *before):
    return lax.optimization_barrier((value, before))[0]


def project_kernel(layout, heads, depth, keep, first, order_ref, *refs):
    count = len(layout)
    own, others, refs = refs[:count], refs[count : 2 * count], refs[2 * count :]
    total = sum(len(p) for p in layout)
    flat, refs = refs[:total], refs[total:]
    acc_in = None
    if not first:
        acc_in, refs = refs[:2], refs[3:]
    acc_own, acc_other, stack, sems = refs
    tokens = acc_own.shape[0]
    copies, weights, at = [], [], 0
    for i, rows in enumerate(layout):
        begin = 0
        for r in rows:
            lo, hi = max(begin, keep[0]), min(begin + r, keep[1])
            if lo < hi:
                copies.append(
                    pltpu.make_async_copy(
                        flat[at].at[pl.ds(lo - begin, hi - lo)],
                        stack.at[order_ref[i] // 2, pl.ds(lo - keep[0], hi - lo)],
                        sems.at[len(copies)],
                    )
                )
                copies[-1].start()
            begin, at = begin + r, at + 1
    at = 0
    for rows in layout:
        parts = [flat[at + p][...] for p in range(len(rows))]
        weights.append(parts[0] if len(parts) == 1 else jnp.concatenate(parts, axis=0))
        at += len(rows)
    for j in range(0, heads, 2):
        wide = min(2, heads - j)
        columns = pl.ds(j * 128, wide * 128)
        total = None
        for i in range(count):
            x = jnp.concatenate([own[i][...], others[i][...]], axis=0)
            w = [weights[i][(j + n) * depth : (j + n + 1) * depth] for n in range(wide)]
            w = w[0] if wide == 1 else jnp.concatenate(w, axis=1)
            term = jnp.dot(x, w, preferred_element_type=F32)
            total = term if total is None else total + term
        mine, theirs = total[:tokens], total[tokens:]
        if not first:
            mine, theirs = mine + acc_in[0][:, columns], theirs + acc_in[1][:, columns]
        acc_own[:, columns] = mine
        acc_other[:, columns] = theirs
    for copy in copies:
        copy.wait()


def project(x, x_other, pieces, order, state, heads, keep, chips):
    tokens, depth = x.shape[0], x_other.shape[1] // chips
    layout = tuple(tuple(p.shape[0] for p in parts) for parts in pieces)
    flat = [p for parts in pieces for p in parts]
    first = state is None
    count = len(pieces)
    whole = pl.BlockSpec(memory_space=pltpu.VMEM)
    anywhere = pl.BlockSpec(memory_space=pl.ANY)

    def block(i, share):
        return pl.BlockSpec((tokens, depth), lambda g, o: (0, o[i] // share))

    x_specs = [block(i, 1) for i in range(count)] + [block(i, 2) for i in range(count)]
    n_in = 1 + 2 * count + len(flat)
    acc = jax.ShapeDtypeStruct((tokens, heads * 128), F32)
    return pl.pallas_call(
        functools.partial(project_kernel, layout, heads, depth, keep, first),
        grid_spec=pltpu.PrefetchScalarGridSpec(
            num_scalar_prefetch=1,
            grid=(1,),
            in_specs=x_specs + [whole] * len(flat) + ([] if first else [whole, whole, anywhere]),
            out_specs=[whole, whole, anywhere],
            scratch_shapes=[pltpu.SemaphoreType.DMA((len(flat),))],
        ),
        out_shape=[acc, acc, jax.ShapeDtypeStruct((chips, keep[1] - keep[0], 128), BF16)],
        input_output_aliases={} if first else {n_in: 0, n_in + 1: 1, n_in + 2: 2},
        compiler_params=pltpu.CompilerParams(vmem_limit_bytes=VMEM_LIMIT),
        name="project",
    )(order, *([x] * count), *([x_other] * count), *flat, *(() if first else state))


def attention_kernel(
    slots, here_ref, q_own, q_more, da_own, da_more, gates, pick, place, kv_own, kv_other,
    dq_out, dkv_out, scores, grads, keys_t,
):
    experts = gates.shape[1]
    width = 128
    tokens = q_own.shape[0]
    here = here_ref[0]
    chip, core = here // 2, here % 2
    scale = width**-0.5
    sides = ((kv_own, core), (kv_other, 1 - core))
    q_parts, da_parts = [], []
    for j in range(experts):
        columns = pl.ds(j * width, width)
        rows = pl.ds(j * slots, slots)
        q_tok = (q_own[:, columns] + q_more[:, columns]).astype(BF16)
        da_tok = da_own[:, columns] + da_more[:, columns]
        da_tok = (gates[:, pl.ds(j, 1)] * da_tok).astype(BF16)
        q_parts.append(jnp.dot(pick[rows, :], q_tok, preferred_element_type=F32))
        da_parts.append(jnp.dot(pick[rows, :], da_tok, preferred_element_type=F32))
    shared = pl.ds(experts * width, width)
    q32 = jnp.concatenate(q_parts + [q_own[:, shared] + q_more[:, shared]], axis=0)
    da32 = jnp.concatenate(da_parts + [da_own[:, shared] + da_more[:, shared]], axis=0)
    q, q_t = q32.astype(BF16), q32.T.astype(BF16)
    da, da_t = da32.astype(BF16), da32.T.astype(BF16)
    count = q.shape[0]
    places = place[...]

    def score(b, top, masked):
        for side, (kv, parity) in enumerate(sides):
            k = kv[b, pl.ds(0, tokens), :]
            s = jnp.dot(k, q_t, preferred_element_type=F32)
            if masked:
                row = (2 * b + parity) * tokens + lax.broadcasted_iota(jnp.int32, s.shape, 0)
                s = jnp.where(row <= places, s, -1e30)
            scores[b, side] = s
            grads[b, side] = jnp.dot(
                kv[b, pl.ds(tokens, tokens), :], da_t, preferred_element_type=F32
            )
            keys_t[b, side] = k.T
            top = jnp.maximum(top, jnp.max(s, axis=0, keepdims=True))
        return top

    top = score(chip, jnp.full((1, count), -3e38, F32), True)
    top = lax.fori_loop(0, chip, lambda b, t: score(b, t, False), top)

    def raise_(b, norm):
        for side in range(2):
            e = jnp.exp2((scores[b, side] - top) * (scale * LOG2E))
            scores[b, side] = e
            norm = norm + jnp.sum(e, axis=0, keepdims=True)
        return norm

    norm = lax.fori_loop(0, chip + 1, raise_, jnp.zeros((1, count), F32))
    inverse = 1.0 / norm

    def values(b, delta):
        for side, (_, parity) in enumerate(sides):
            low = (scores[b, side] * inverse).astype(BF16)
            dkv_out[2 * b + parity, pl.ds(tokens, tokens), :] = jnp.dot(
                low, da, preferred_element_type=F32
            ).astype(BF16)
            delta = delta + jnp.sum(low.astype(F32) * grads[b, side], axis=0, keepdims=True)
        return delta

    delta = lax.fori_loop(0, chip + 1, values, jnp.zeros((1, count), F32))
    factor = inverse * scale

    def keys(b, dq_t):
        for side, (_, parity) in enumerate(sides):
            ds = (scores[b, side] * (grads[b, side] - delta) * factor).astype(BF16)
            dkv_out[2 * b + parity, pl.ds(0, tokens), :] = jnp.dot(
                ds, q, preferred_element_type=F32
            ).astype(BF16)
            dq_t = dq_t + jnp.dot(keys_t[b, side], ds, preferred_element_type=F32)
        return dq_t

    dq_t = lax.fori_loop(0, chip + 1, keys, jnp.zeros((width, count), F32)).astype(BF16)

    def blank(b, carry):
        dkv_out[b] = jnp.zeros(dkv_out.shape[1:], BF16)
        return carry

    lax.fori_loop(2 * chip + 2, dkv_out.shape[0], blank, 0)
    for j in range(0, experts, 2):
        both = dq_t[:, j * slots : (j + 2) * slots]
        for n in range(2):
            lane = lax.broadcasted_iota(jnp.int32, both.shape, 1)
            part = jnp.where(lane // slots == n, both, jnp.zeros_like(both))
            dq_out[pl.ds((j + n) * width, width), :] = jnp.dot(
                part, pick[pl.ds(j * slots, 2 * slots), :], preferred_element_type=F32
            ).astype(BF16)
    dq_out[pl.ds(experts * width, width), :] = dq_t[:, experts * slots :]


def attention(slots, here, q_own, q_more, da_own, da_more, gates, pick, place, kv_own, kv_other):
    tokens, chips = q_own.shape[0], kv_own.shape[0]
    count = place.shape[1]
    whole = pl.BlockSpec(memory_space=pltpu.VMEM)
    return pl.pallas_call(
        functools.partial(attention_kernel, slots),
        in_specs=[pl.BlockSpec(memory_space=pltpu.SMEM)] + [whole] * 9,
        out_specs=[whole, whole],
        out_shape=[
            jax.ShapeDtypeStruct((q_own.shape[1], tokens), BF16),
            jax.ShapeDtypeStruct((2 * chips, 2 * tokens, 128), BF16),
        ],
        scratch_shapes=[
            pltpu.VMEM((chips, 2, tokens, count), F32),
            pltpu.VMEM((chips, 2, tokens, count), F32),
            pltpu.VMEM((chips, 2, 128, tokens), BF16),
        ],
        compiler_params=pltpu.CompilerParams(vmem_limit_bytes=VMEM_LIMIT),
        name="attention",
    )(here, q_own, q_more, da_own, da_more, gates, pick, place, kv_own, kv_other)


def back_kernel(heads, depth, count, order_ref, core_ref, dq_t, own, other, out, weights, sems):
    for i in range(count):
        block = order_ref[i]
        mine = block % 2 == core_ref[0]

        @pl.when(mine)
        def _():
            pltpu.make_async_copy(own.at[block // 2], weights.at[i], sems.at[i]).start()

        @pl.when(jnp.logical_not(mine))
        def _():
            pltpu.make_async_copy(other.at[block // 2], weights.at[i], sems.at[i]).start()

    for i in range(count):
        pltpu.make_async_copy(own.at[0], weights.at[i], sems.at[i]).wait()
        total = None
        for j in range(0, heads, 2):
            wide = min(2, heads - j)
            w = [weights[i, pl.ds((j + n) * depth, depth), :] for n in range(wide)]
            w = w[0] if wide == 1 else jnp.concatenate(w, axis=1)
            term = jnp.dot(
                w, dq_t[pl.ds(j * 128, wide * 128), :], preferred_element_type=F32
            )
            total = term if total is None else total + term
        out[i] = total.astype(BF16)


def back_project(dq_t, own, other, order, core, heads):
    tokens, depth, count = dq_t.shape[1], own.shape[1] // heads, order.shape[0]
    whole = pl.BlockSpec(memory_space=pltpu.VMEM)
    scalar = pl.BlockSpec(memory_space=pltpu.SMEM)
    anywhere = pl.BlockSpec(memory_space=pl.ANY)
    return pl.pallas_call(
        functools.partial(back_kernel, heads, depth, count),
        in_specs=[scalar, scalar, whole, anywhere, anywhere],
        out_specs=whole,
        out_shape=jax.ShapeDtypeStruct((count, depth, tokens), BF16),
        scratch_shapes=[
            pltpu.VMEM((count,) + own.shape[1:], BF16),
            pltpu.SemaphoreType.DMA((count,)),
        ],
        compiler_params=pltpu.CompilerParams(vmem_limit_bytes=VMEM_LIMIT),
        name="back_project",
    )(order, core, dq_t, own, other)


def plus(*terms):
    return sum(t.astype(F32) for t in terms)


def per_device(
    layer_input, output_grad, routes, route_gates, query_weight, output_weight, key_values
):
    tokens = layer_input.shape[0]
    heads = query_weight.shape[0]
    experts = heads - 1
    depth, width = query_weight.shape[1:]
    blocks = lax.axis_size("ctx")
    head_count = lax.axis_size("head")
    slots = 2 * tokens * routes.shape[1] // (experts * head_count)
    c = lax.axis_index("ctx")
    h = lax.axis_index("head")
    z, x, k = c // (2 * NX), (c // 2) % NX, c % 2
    y, zh = h // NZ, h % NZ
    is_even = h % 2 == 0

    core_only = k.astype(jnp.int32)[None]

    def blocks_of(*chips):
        return jnp.stack([ctx_id(z ^ dz, x + dx + NX, k) for dz, dx in chips]).astype(jnp.int32)

    rows = heads * depth
    wq = query_weight.reshape(rows, width)
    q_left, q_right, q_below = (ctx_send(wq, m) for m in (X_UP, X_DOWN, Z_PAIR))
    own_rows = key_values[0]
    partner_rows = lax.ppermute(own_rows, "head", HEAD_PAIR)

    def other_half(value):
        split = value.reshape(tokens, blocks // 2, 2, depth)
        half = jnp.where(k == 0, split[:, :, 1], split[:, :, 0])
        return ctx_send(half.reshape(tokens, blocks // 2 * depth), CORES)

    x_other = other_half(layer_input)
    g_other = other_half(output_grad)
    wo = jnp.concatenate(
        [
            output_weight.reshape(rows, width),
            jnp.where(is_even, own_rows, partner_rows),
            jnp.where(is_even, partner_rows, own_rows),
        ],
        axis=0,
    )
    o_left, o_right, o_below = (ctx_send(wo, m) for m in (X_UP, X_DOWN, Z_PAIR))

    ids = h * experts + jnp.arange(experts, dtype=jnp.int32)
    matches = routes[:, :, None] == ids[None, None, :]
    member = jnp.any(matches, axis=1)
    gates = jnp.sum(jnp.where(matches, route_gates[:, :, None], 0.0), axis=1)
    index = jnp.arange(tokens, dtype=jnp.int32)
    before = (index[None, :] <= index[:, None]).astype(BF16)
    placed = jnp.dot(before, member.astype(BF16), preferred_element_type=F32)
    placed = placed.astype(jnp.int32) - 1
    table = (placed.T[:, None, :] == jnp.arange(slots, dtype=jnp.int32)[None, :, None]) & (
        member.T[:, None, :]
    )
    token_place = c * tokens + index
    routed_place = jnp.max(jnp.where(table, token_place[None, None, :], c * tokens), axis=2)
    place = jnp.concatenate([routed_place.reshape(-1), token_place])[None, :]
    pick = table.reshape(experts * slots, tokens).astype(BF16)
    near, far = blocks_of((0, 0), (0, -1), (0, 1), (1, 0)), blocks_of((0, 2))
    last, most = blocks_of((1, -1), (1, 1), (1, 2)), blocks_of((0, 2), (1, -1), (1, 1), (1, 2))
    z_order = (zh + jnp.array([2, 1, 3, 0], jnp.int32)) % NZ
    y_order = (y + jnp.array([2, 1, 3, 0], jnp.int32)) % NY
    grid = (y_order[:, None] * NZ + z_order[None, :]).astype(jnp.int32)

    chips = blocks // 2
    keep_q, keep_o = (0, rows), (rows, rows + 2 * tokens)
    q_half, o_half = wq.shape[0] // 2, wo.shape[0] // 2
    q_left_, q_right_ = after((q_left, q_right), pick, place, gates, near, most)
    q_far_a = ctx_send(q_left_[:q_half], X_UP)
    q_far_b = ctx_send(q_right_[q_half:], X_DOWN)
    state_q = project(
        layer_input,
        x_other,
        [(wq,), (q_left_,), (q_right_,), (q_below,)],
        near,
        None,
        heads,
        keep_q,
        chips,
    )
    o_left_, o_right_, q_below_ = after((o_left, o_right, q_below), state_q[0])
    o_far_a = ctx_send(o_left_[:o_half], X_UP)
    o_far_b = ctx_send(o_right_[o_half:], X_DOWN)
    q_diag_l, q_diag_r = ctx_send(q_below_, X_UP), ctx_send(q_below_, X_DOWN)
    q_corner_a, q_corner_b = ctx_send(q_far_a, Z_PAIR), ctx_send(q_far_b, Z_PAIR)
    state_o = project(
        output_grad,
        g_other,
        [(wo,), (o_left_,), (o_right_,), (o_below,)],
        near,
        None,
        heads,
        keep_o,
        chips,
    )
    o_far_a_, o_far_b_, o_below_ = after((o_far_a, o_far_b, o_below), state_o[0])
    o_corner_a, o_corner_b = ctx_send(o_far_a_, Z_PAIR), ctx_send(o_far_b_, Z_PAIR)
    o_diag_l, o_diag_r = ctx_send(o_below_, X_UP), ctx_send(o_below_, X_DOWN)
    q_own, q_theirs, q_stack = project(
        layer_input,
        x_other,
        [(q_far_a, q_far_b), (q_diag_l,), (q_diag_r,), (q_corner_a, q_corner_b)],
        most,
        state_q,
        heads,
        keep_q,
        chips,
    )
    q_more = ctx_send(q_theirs, CORES)
    q_stack_other = ctx_send(q_stack, CORES)
    state_o = project(
        output_grad, g_other, [(o_far_a_, o_far_b_)], far, state_o, heads, keep_o, chips
    )
    da_own, da_theirs, kv_own = project(
        output_grad,
        g_other,
        [(o_diag_l,), (o_diag_r,), (o_corner_a, o_corner_b)],
        last,
        after(state_o, q_own),
        heads,
        keep_o,
        chips,
    )
    da_more = ctx_send(da_theirs, CORES)
    kv_other = ctx_send(kv_own, CORES)
    dq_t, dkv = attention(
        slots,
        c.astype(jnp.int32)[None],
        q_own,
        q_more,
        da_own,
        da_more,
        gates,
        pick,
        place,
        kv_own,
        kv_other,
    )

    def terms(*places):
        order = jnp.stack([grid[p] for p in places])
        return back_project(dq_t, q_stack, q_stack_other, order, core_only, heads)

    def up(value):
        return lax.ppermute(value, "head", head_moves(1, 0))

    def down(value):
        return lax.ppermute(value, "head", head_moves(-1, 0))

    sums = []
    sent = None
    for s in (0, 2):
        u = terms((0, s), (1, s + 1))
        u_in = up(u)
        d = terms((0, s + 1), (2, s))
        d_in = down(d)
        rest = terms((1, s), (2, s + 1), (3, s), (3, s + 1))
        u2_in = up(plus(rest[0], u_in[0]).astype(BF16))
        d2_in = down(plus(rest[1], d_in[0]).astype(BF16))
        sums.append(plus(rest[2], u2_in, d_in[1]))
        sums.append(plus(rest[3], u_in[1], d2_in))
        sent = rest
    z_in = [
        lax.ppermute(v.astype(BF16), "head", head_moves(0, d))
        for v, d in zip(sums[:3], (2, 1, -1), strict=True)
    ]
    input_grad = plus(sums[3], *z_in).T.astype(BF16)

    dkv = after(dkv, sent)
    arrived = lax.all_to_all(dkv, "ctx", split_axis=0, concat_axis=0, tiled=True)
    summed = jnp.sum(arrived.astype(F32), axis=0)
    key_rows, value_rows = summed[:tokens], summed[tokens:]
    incoming = lax.ppermute(jnp.where(is_even, value_rows, key_rows), "head", HEAD_PAIR)
    kept = jnp.where(is_even, key_rows, value_rows) + incoming
    return input_grad, kept[None]


def solution(mesh):
    in_specs = (
        P("ctx", None),
        P("ctx", None),
        P("ctx", None),
        P("ctx", None),
        P("head", "ctx", None),
        P("head", "ctx", None),
        P("head", "ctx", None),
    )
    out_specs = (P("ctx", "head"), P("head", "ctx", None))
    return jax.shard_map(
        per_device, mesh=mesh, in_specs=in_specs, out_specs=out_specs, check_vma=False
    )
```

```python
import functools

import jax
import jax.numpy as jnp
from jax import lax
from jax.experimental import pallas as pl
from jax.experimental.pallas import tpu as pltpu
from jax.sharding import PartitionSpec as P

F32 = jnp.float32
BF16 = jnp.bfloat16
VMEM_LIMIT = 56 * 2**20
LOG2E = 1.4426950408889634

NX, NY, NZ = 4, 4, 4


def ctx_id(z, x, k):
    return z * 2 * NX + (x % NX) * 2 + k


def ctx_moves(target):
    return [
        (ctx_id(z, x, k), target(z, x, k)) for z in range(2) for x in range(NX) for k in range(2)
    ]


X_UP = ctx_moves(lambda z, x, k: ctx_id(z, x + 1, k))
X_DOWN = ctx_moves(lambda z, x, k: ctx_id(z, x - 1, k))
Z_PAIR = ctx_moves(lambda z, x, k: ctx_id(1 - z, x, k))
CORES = ctx_moves(lambda z, x, k: ctx_id(z, x, 1 - k))


def head_moves(dy, dz):
    return [
        (y * NZ + z, ((y + dy) % NY) * NZ + (z + dz) % NZ) for y in range(NY) for z in range(NZ)
    ]


HEAD_PAIR = [(h, h ^ 1) for h in range(NY * NZ)]


def cost(flops, bytes_accessed, exps=0):
    return pl.CostEstimate(flops=flops, bytes_accessed=bytes_accessed, transcendentals=exps)


def ctx_send(value, moves):
    return lax.ppermute(value, "ctx", moves)


def after(value, *before):
    return lax.optimization_barrier((value, before))[0]


def pack_kernel(place_ref, x, out):
    out[...] = x[...]


def pack_other_half(x, place, chips):
    tokens, depth = x.shape[0], x.shape[1] // (2 * chips)
    return pl.pallas_call(
        pack_kernel,
        grid_spec=pltpu.PrefetchScalarGridSpec(
            num_scalar_prefetch=1,
            grid=(chips,),
            in_specs=[pl.BlockSpec((tokens, depth), lambda i, p: (0, 2 * i + 1 - p[2]))],
            out_specs=pl.BlockSpec((tokens, depth), lambda i, p: (0, i)),
        ),
        out_shape=jax.ShapeDtypeStruct((tokens, chips * depth), x.dtype),
        cost_estimate=cost(0, 2 * tokens * chips * depth * 2),
        name="pack_half",
    )(place, x)


def chip_of(place_ref, offset):
    dz, dx = offset
    return (place_ref[0] ^ dz) * NX + lax.rem(place_ref[1] + dx + NX, NX)


def project_kernel(layout, heads, depth, keep, first, place_ref, *refs):
    count = len(layout)
    xs = [refs[i * count : (i + 1) * count] for i in range(4)]
    total = 1 + max(seg[0] for _, segs in layout for seg in segs)
    flat, refs = refs[4 * count : 4 * count + total], refs[4 * count + total :]
    acc_in = None
    if not first:
        acc_in, refs = refs[:2], refs[4:]
    acc_own, acc_other, w_stack, kv_stack, sems = refs
    tokens, rows = acc_own.shape[0], heads * depth
    copies = []
    for offset, segs in layout:
        chip = chip_of(place_ref, offset)
        for stack, begin, end in ((w_stack, 0, rows), (kv_stack, 2 * rows, 2 * rows + keep)):
            for ref, at, row, n in segs:
                lo, hi = max(begin, row), min(end, row + n)
                if lo < hi:
                    copies.append(
                        pltpu.make_async_copy(
                            flat[ref].at[pl.ds(at + lo - row, hi - lo)],
                            stack.at[chip, pl.ds(lo - begin, hi - lo)],
                            sems.at[len(copies)],
                        )
                    )
                    copies[-1].start()

    def weight(segs, begin):
        end, parts = begin + depth, []
        for ref, at, row, n in segs:
            lo, hi = max(begin, row), min(end, row + n)
            if lo < hi:
                parts.append(flat[ref][pl.ds(at + lo - row, hi - lo), :])
        return parts[0] if len(parts) == 1 else jnp.concatenate(parts, axis=0)

    for side in range(2):
        own, others = xs[2 * side], xs[2 * side + 1]
        for j in range(0, heads, 2):
            wide = min(2, heads - j)
            columns = pl.ds((side * heads + j) * 128, wide * 128)
            total = None
            for i, (_, segs) in enumerate(layout):
                x = jnp.concatenate([own[i][...], others[i][...]], axis=0)
                w = [weight(segs, side * rows + (j + n) * depth) for n in range(wide)]
                w = w[0] if wide == 1 else jnp.concatenate(w, axis=1)
                term = jnp.dot(x, w, preferred_element_type=F32)
                total = term if total is None else total + term
            mine, theirs = total[:tokens], total[tokens:]
            if not first:
                mine, theirs = mine + acc_in[0][:, columns], theirs + acc_in[1][:, columns]
            acc_own[:, columns] = mine
            acc_other[:, columns] = theirs
    for copy in copies:
        copy.wait()


def project(xs, arrays, layout, place, state, heads, keep, chips):
    tokens, depth = xs[0].shape[0], xs[1].shape[1] // chips
    first = state is None
    count = len(layout)
    whole = pl.BlockSpec(memory_space=pltpu.VMEM)
    anywhere = pl.BlockSpec(memory_space=pl.ANY)

    def mine(o):
        return pl.BlockSpec((tokens, depth), lambda g, p: (0, 2 * chip_of(p, o) + p[2]))

    def theirs(o):
        return pl.BlockSpec((tokens, depth), lambda g, p: (0, chip_of(p, o)))

    offsets = [o for o, _ in layout]
    n_in = 1 + 4 * count + len(arrays)
    acc = jax.ShapeDtypeStruct((tokens, 2 * heads * 128), F32)
    copies = sum(len(segs) for _, segs in layout) * 2
    return pl.pallas_call(
        functools.partial(project_kernel, layout, heads, depth, keep, first),
        grid_spec=pltpu.PrefetchScalarGridSpec(
            num_scalar_prefetch=1,
            grid=(1,),
            in_specs=([mine(o) for o in offsets] + [theirs(o) for o in offsets]) * 2
            + [whole] * len(arrays)
            + ([] if first else [whole, whole, anywhere, anywhere]),
            out_specs=[whole, whole, anywhere, anywhere],
            scratch_shapes=[pltpu.SemaphoreType.DMA((copies,))],
        ),
        out_shape=[
            acc,
            acc,
            jax.ShapeDtypeStruct((chips, heads * depth, 128), BF16),
            jax.ShapeDtypeStruct((chips, keep, 128), BF16),
        ],
        input_output_aliases={} if first else {n_in + i: i for i in range(4)},
        compiler_params=pltpu.CompilerParams(vmem_limit_bytes=VMEM_LIMIT),
        cost_estimate=cost(
            8 * tokens * depth * heads * 128 * count,
            count * (4 * heads * depth * 128 + 4 * tokens * depth) * 2 + 8 * tokens * heads * 512,
        ),
        name="project",
    )(
        place,
        *[x for x in xs for _ in range(count)],
        *arrays,
        *(() if first else state),
    )


def attention_kernel(
    slots, here_ref, own, more, gates, pick, place, kv_own, kv_other,
    dq_out, dkv_out, scores, grads, keys_t,
):
    experts = gates.shape[1]
    width = 128
    tokens = own.shape[0]
    heads = experts + 1
    core = here_ref[2]
    chip = here_ref[0] * NX + here_ref[1]
    scale = width**-0.5
    sides = ((kv_own, core), (kv_other, 1 - core))
    q_parts, da_parts = [], []
    for j in range(experts):
        columns, da_columns = pl.ds(j * width, width), pl.ds((heads + j) * width, width)
        rows = pl.ds(j * slots, slots)
        q_tok = (own[:, columns] + more[:, columns]).astype(BF16)
        da_tok = own[:, da_columns] + more[:, da_columns]
        da_tok = (gates[:, pl.ds(j, 1)] * da_tok).astype(BF16)
        q_parts.append(jnp.dot(pick[rows, :], q_tok, preferred_element_type=F32))
        da_parts.append(jnp.dot(pick[rows, :], da_tok, preferred_element_type=F32))
    shared, da_shared = pl.ds(experts * width, width), pl.ds((heads + experts) * width, width)
    q32 = jnp.concatenate(q_parts + [own[:, shared] + more[:, shared]], axis=0)
    da32 = jnp.concatenate(da_parts + [own[:, da_shared] + more[:, da_shared]], axis=0)
    q, q_t = q32.astype(BF16), q32.T.astype(BF16)
    da, da_t = da32.astype(BF16), da32.T.astype(BF16)
    count = q.shape[0]
    places = place[...]

    def score(b, top, masked):
        for side, (kv, parity) in enumerate(sides):
            k = kv[b, pl.ds(0, tokens), :]
            s = jnp.dot(k, q_t, preferred_element_type=F32)
            if masked:
                row = (2 * b + parity) * tokens + lax.broadcasted_iota(jnp.int32, s.shape, 0)
                s = jnp.where(row <= places, s, -1e30)
            scores[b, side] = s
            grads[b, side] = jnp.dot(
                kv[b, pl.ds(tokens, tokens), :], da_t, preferred_element_type=F32
            )
            keys_t[b, side] = k.T
            top = jnp.maximum(top, jnp.max(s, axis=0, keepdims=True))
        return top

    top = score(chip, jnp.full((1, count), -3e38, F32), True)
    top = lax.fori_loop(0, chip, lambda b, t: score(b, t, False), top)

    def raise_(b, norm):
        for side in range(2):
            e = jnp.exp2((scores[b, side] - top) * (scale * LOG2E))
            scores[b, side] = e
            norm = norm + jnp.sum(e, axis=0, keepdims=True)
        return norm

    norm = lax.fori_loop(0, chip + 1, raise_, jnp.zeros((1, count), F32))
    inverse = 1.0 / norm

    def values(b, delta):
        for side, (_, parity) in enumerate(sides):
            low = (scores[b, side] * inverse).astype(BF16)
            dkv_out[2 * b + parity, pl.ds(tokens, tokens), :] = jnp.dot(
                low, da, preferred_element_type=F32
            ).astype(BF16)
            delta = delta + jnp.sum(low.astype(F32) * grads[b, side], axis=0, keepdims=True)
        return delta

    delta = lax.fori_loop(0, chip + 1, values, jnp.zeros((1, count), F32))
    factor = inverse * scale

    def keys(b, dq_t):
        for side, (_, parity) in enumerate(sides):
            ds = (scores[b, side] * (grads[b, side] - delta) * factor).astype(BF16)
            dkv_out[2 * b + parity, pl.ds(0, tokens), :] = jnp.dot(
                ds, q, preferred_element_type=F32
            ).astype(BF16)
            dq_t = dq_t + jnp.dot(keys_t[b, side], ds, preferred_element_type=F32)
        return dq_t

    dq_t = lax.fori_loop(0, chip + 1, keys, jnp.zeros((width, count), F32)).astype(BF16)

    def blank(b, carry):
        dkv_out[b] = jnp.zeros(dkv_out.shape[1:], BF16)
        return carry

    lax.fori_loop(2 * chip + 2, dkv_out.shape[0], blank, 0)
    for j in range(0, experts, 2):
        both = dq_t[:, j * slots : (j + 2) * slots]
        for n in range(2):
            lane = lax.broadcasted_iota(jnp.int32, both.shape, 1)
            part = jnp.where(lane // slots == n, both, jnp.zeros_like(both))
            dq_out[pl.ds((j + n) * width, width), :] = jnp.dot(
                part, pick[pl.ds(j * slots, 2 * slots), :], preferred_element_type=F32
            ).astype(BF16)
    dq_out[pl.ds(experts * width, width), :] = dq_t[:, experts * slots :]


def attention(slots, here, own, more, gates, pick, place, kv_own, kv_other):
    tokens, chips = own.shape[0], kv_own.shape[0]
    count = place.shape[1]
    whole = pl.BlockSpec(memory_space=pltpu.VMEM)
    return pl.pallas_call(
        functools.partial(attention_kernel, slots),
        in_specs=[pl.BlockSpec(memory_space=pltpu.SMEM)] + [whole] * 7,
        out_specs=[whole, whole],
        out_shape=[
            jax.ShapeDtypeStruct((own.shape[1] // 2, tokens), BF16),
            jax.ShapeDtypeStruct((2 * chips, 2 * tokens, 128), BF16),
        ],
        scratch_shapes=[
            pltpu.VMEM((chips, 2, tokens, count), F32),
            pltpu.VMEM((chips, 2, tokens, count), F32),
            pltpu.VMEM((chips, 2, 128, tokens), BF16),
        ],
        compiler_params=pltpu.CompilerParams(vmem_limit_bytes=VMEM_LIMIT),
        cost_estimate=cost(
            20 * chips * tokens * count * 128, 8 * chips * tokens * 128 * 2, 2 * chips * tokens * count
        ),
        name="attention",
    )(here, own, more, gates, pick, place, kv_own, kv_other)


def back_kernel(heads, depth, spots, place_ref, dq_t, own, other, *refs):
    outs, (weights, sems) = refs[:-2], refs[-2:]
    flat = [(o, i, spot) for o, group in zip(outs, spots, strict=True) for i, spot in enumerate(group)]
    for n, (_, _, (dy, dz)) in enumerate(flat):
        block = lax.rem(place_ref[3] + dy, NY) * NZ + lax.rem(place_ref[4] + dz, NZ)
        mine = lax.rem(block, 2) == place_ref[2]

        @pl.when(mine)
        def _():
            pltpu.make_async_copy(own.at[block // 2], weights.at[n], sems.at[n]).start()

        @pl.when(jnp.logical_not(mine))
        def _():
            pltpu.make_async_copy(other.at[block // 2], weights.at[n], sems.at[n]).start()

    for n, (out, i, _) in enumerate(flat):
        pltpu.make_async_copy(own.at[0], weights.at[n], sems.at[n]).wait()
        total = None
        for j in range(0, heads, 2):
            wide = min(2, heads - j)
            w = [weights[n, pl.ds((j + m) * depth, depth), :] for m in range(wide)]
            w = w[0] if wide == 1 else jnp.concatenate(w, axis=1)
            term = jnp.dot(w, dq_t[pl.ds(j * 128, wide * 128), :], preferred_element_type=F32)
            total = term if total is None else total + term
        out[i] = total.astype(BF16)


def back_project(dq_t, own, other, place, spots, heads):
    tokens, depth = dq_t.shape[1], own.shape[1] // heads
    count = sum(len(group) for group in spots)
    whole = pl.BlockSpec(memory_space=pltpu.VMEM)
    anywhere = pl.BlockSpec(memory_space=pl.ANY)
    return pl.pallas_call(
        functools.partial(back_kernel, heads, depth, spots),
        in_specs=[pl.BlockSpec(memory_space=pltpu.SMEM), whole, anywhere, anywhere],
        out_specs=[whole] * len(spots),
        out_shape=[jax.ShapeDtypeStruct((len(g), depth, tokens), BF16) for g in spots],
        scratch_shapes=[
            pltpu.VMEM((count,) + own.shape[1:], BF16),
            pltpu.SemaphoreType.DMA((count,)),
        ],
        compiler_params=pltpu.CompilerParams(vmem_limit_bytes=VMEM_LIMIT),
        cost_estimate=cost(
            2 * count * tokens * depth * heads * 128,
            count * (heads * depth * 128 + depth * tokens) * 2 + dq_t.size * 2,
        ),
        name="back_project",
    )(place, dq_t, own, other)


def plus(*terms):
    return sum(t.astype(F32) for t in terms)


def per_device(
    layer_input, output_grad, routes, route_gates, query_weight, output_weight, key_values
):
    tokens = layer_input.shape[0]
    heads = query_weight.shape[0]
    experts = heads - 1
    depth, width = query_weight.shape[1:]
    blocks = lax.axis_size("ctx")
    head_count = lax.axis_size("head")
    slots = 2 * tokens * routes.shape[1] // (experts * head_count)
    c = lax.axis_index("ctx")
    h = lax.axis_index("head")
    z, x, k = c // (2 * NX), (c // 2) % NX, c % 2
    y, zh = h // NZ, h % NZ
    is_even = h % 2 == 0

    place = jnp.stack([z, x, k, y, zh]).astype(jnp.int32)
    chips = blocks // 2

    rows = heads * depth
    wq = query_weight.reshape(rows, width)
    q_left, q_right, q_below = (ctx_send(wq, m) for m in (X_UP, X_DOWN, Z_PAIR))
    own_rows = key_values[0]
    partner_rows = lax.ppermute(own_rows, "head", HEAD_PAIR)
    x_other = ctx_send(pack_other_half(layer_input, place, chips), CORES)
    g_other = ctx_send(pack_other_half(output_grad, place, chips), CORES)
    wo = jnp.concatenate(
        [
            output_weight.reshape(rows, width),
            jnp.where(is_even, own_rows, partner_rows),
            jnp.where(is_even, partner_rows, own_rows),
        ],
        axis=0,
    )
    o_left, o_right, o_below = (ctx_send(wo, m) for m in (X_UP, X_DOWN, Z_PAIR))

    ids = h * experts + jnp.arange(experts, dtype=jnp.int32)
    matches = routes[:, :, None] == ids[None, None, :]
    member = jnp.any(matches, axis=1)
    gates = jnp.sum(jnp.where(matches, route_gates[:, :, None], 0.0), axis=1)
    index = jnp.arange(tokens, dtype=jnp.int32)
    before = (index[None, :] <= index[:, None]).astype(BF16)
    placed = jnp.dot(before, member.astype(BF16), preferred_element_type=F32)
    placed = placed.astype(jnp.int32) - 1
    table = (placed.T[:, None, :] == jnp.arange(slots, dtype=jnp.int32)[None, :, None]) & (
        member.T[:, None, :]
    )
    token_place = c * tokens + index
    routed_place = jnp.max(jnp.where(table, token_place[None, None, :], c * tokens), axis=2)
    position = jnp.concatenate([routed_place.reshape(-1), token_place])[None, :]
    pick = table.reshape(experts * slots, tokens).astype(BF16)

    keep = 2 * tokens
    n_q, n_o = rows, rows + keep
    h_q, h_o = n_q // 2, n_o // 2

    def split(a, b):
        return ((a, 0, 0, n_q), (b, 0, n_q, n_o))

    def halves(a, b):
        return (
            (a, 0, 0, h_q),
            (b, 0, h_q, h_q),
            (a, h_q, n_q, h_o),
            (b, h_q, n_q + h_o, h_o),
        )

    def add(arrays, layout, state):
        xs = (layer_input, x_other, output_grad, g_other)
        return project(xs, arrays, layout, place, state, heads, keep, chips)

    near = (q_left, q_right, q_below, o_left, o_right, o_below)
    near = after(near, pick, position, gates, x_other, g_other)
    q_left, q_right, q_below, o_left, o_right, o_below = near
    far_a = ctx_send(jnp.concatenate([q_left[:h_q], o_left[:h_o]], axis=0), X_UP)
    far_b = ctx_send(jnp.concatenate([q_right[h_q:], o_right[h_o:]], axis=0), X_DOWN)
    state = add(
        (wq, wo, q_left, o_left, q_right, o_right, q_below, o_below),
        (
            ((0, 0), split(0, 1)),
            ((0, -1), split(2, 3)),
            ((0, 1), split(4, 5)),
            ((1, 0), split(6, 7)),
        ),
        None,
    )
    below = jnp.concatenate([q_below, o_below], axis=0)

    far_a, far_b, below = after((far_a, far_b, below), state[0])
    left, right = ctx_send(below, X_UP), ctx_send(below, X_DOWN)
    corner_a, corner_b = ctx_send(far_a, Z_PAIR), ctx_send(far_b, Z_PAIR)
    state = add((far_a, far_b), (((0, 2), halves(0, 1)),), state)
    every = ((0, 0, 0, n_q + n_o),)
    own, theirs, q_stack, kv_own = add(
        (left, right, corner_a, corner_b),
        (
            ((1, -1), every),
            ((1, 1), ((1, 0, 0, n_q + n_o),)),
            ((1, 2), halves(2, 3)),
        ),
        state,
    )
    more = ctx_send(theirs, CORES)
    kv_other = ctx_send(kv_own, CORES)
    q_stack_other = ctx_send(after(q_stack, more, kv_other), CORES)
    dq_t, dkv = attention(slots, place, own, more, gates, pick, position, kv_own, kv_other)

    def spots(near_z, far_z):
        up_first = ((2, near_z), (1, far_z))
        down_first = ((2, far_z), (3, near_z))
        rest = ((1, near_z), (3, far_z), (0, near_z), (0, far_z))
        return up_first, down_first, rest

    def back(dq, *groups):
        return back_project(dq, q_stack, q_stack_other, place, groups, heads)

    def up(value):
        return lax.ppermute(value, "head", head_moves(1, 0))

    def down(value):
        return lax.ppermute(value, "head", head_moves(-1, 0))

    up_a, down_a, rest_a = spots(2, 1)
    up_b, down_b, rest_b = spots(3, 0)
    u_a, d_a = back(dq_t, up_a, down_a)
    r_a, u_b, d_b = back(after(dq_t, u_a), rest_a, up_b, down_b)
    (r_b,) = back(after(dq_t, r_a), rest_b)

    def chunk(u, d, rest):
        u_in, d_in = up(u), down(d)
        u2_in = up(plus(rest[0], u_in[0]).astype(BF16))
        d2_in = down(plus(rest[1], d_in[0]).astype(BF16))
        return plus(rest[2], u2_in, d_in[1]), plus(rest[3], u_in[1], d2_in), d_in

    z_two, z_up, first_in = chunk(u_a, d_a, r_a)
    z_down, z_here, _ = chunk(u_b, d_b, r_b)

    arrived = lax.all_to_all(after(dkv, first_in), "ctx", split_axis=0, concat_axis=0, tiled=True)
    summed = jnp.sum(arrived.astype(F32), axis=0)
    key_rows, value_rows = summed[:tokens], summed[tokens:]
    incoming = lax.ppermute(jnp.where(is_even, value_rows, key_rows), "head", HEAD_PAIR)
    kept = jnp.where(is_even, key_rows, value_rows) + incoming

    z_two, z_up, z_down = after((z_two, z_up, z_down), kept)
    z_in = [
        lax.ppermute(v.astype(BF16), "head", head_moves(0, d))
        for v, d in ((z_two, 2), (z_up, 1), (z_down, -1))
    ]
    input_grad = plus(z_here, *z_in).T.astype(BF16)
    return input_grad, kept[None]


def solution(mesh):
    in_specs = (
        P("ctx", None),
        P("ctx", None),
        P("ctx", None),
        P("ctx", None),
        P("head", "ctx", None),
        P("head", "ctx", None),
        P("head", "ctx", None),
    )
    out_specs = (P("ctx", "head"), P("head", "ctx", None))
    return jax.shard_map(
        per_device, mesh=mesh, in_specs=in_specs, out_specs=out_specs, check_vma=False
    )
```
